512 devices in a mesh: segment: 8 (over x, core), adapter: 64 (over z, y).
Axes of the slice: x: 4, y: 8, z: 8, core: 2. Of those that a mesh axis runs over, the one named last changes fastest.
Arguments:
- incoming: bfloat16 [4096, 8192], P(('segment', 'adapter')), may hold values from -6 to 6
- attention_norm_gain: float32 [8, 8192], P('segment'), may hold values from 0.1 to 1.9
- query_weight: bfloat16 [8, 8192, 8192], P('segment', None, 'adapter'), may hold values from -0.0625 to 0.0625
- adapter_down_weight: bfloat16 [8, 64, 8192, 64], P('segment', 'adapter'), may hold values from -0.0625 to 0.0625
- adapter_up_weight: bfloat16 [8, 64, 64, 8192], P('segment', None, None, 'adapter'), may hold values from -0.75 to 0.75
- request_adapter_index: int32 [4096], P('segment'), may hold values from 0 to 63, as said below
- cache_valid_length: int32 [4096], P('segment'), may hold values from 1 to 16
- key_value_cache: bfloat16 [4096, 2, 16, 1024], P(('segment', 'adapter')), may hold values from -1500 to 1500, as said below
Outputs:
- context: bfloat16 [4096, 8192], P(('segment', 'adapter'))
The draws below stay inside these ranges and needn't reach their ends.
Inputs may be any that keep to these rules, and one draw needn't show every extreme that they name: `request_adapter_index`: adapter a is owned by index a // 1 of adapter. At most 32 of the 512 requests of one section name adapters of one owner, and in every section some owner has exactly 32. `key_value_cache`: positions at or after a request's length hold unused entries.
All inputs are finite; a program needn't handle non-finite values.
Results may differ from the reference program's by a relative error of at most 0.04.
Values may be sent and summed in bfloat16 or wider, within the bound.
No kernel may reach another device: no remote copies, remote signals or barrier semaphores. Data moves between devices by JAX's collectives and lax.ppermute only.
A program may use at most 64 MiB of HBM per device.

```python
import jax
import jax.numpy as jnp
from jax import lax

MODEL_WIDTH = 8192
HEADS = 64
KVH = 8
HD = 128
ADAPTER_RANK = 64
AD_DEV = 1
TOK_DEV = 8
CTX = 16
ROWS = 4096
ADAPTER_COUNT = 64
OWN_MAX = 32
N_SEGMENT = 8
N_ADAPTER = 64


def draw_request_adapter_index(key, part):
    segment_rows = TOK_DEV * N_ADAPTER

    def single_section_part(segment_key):
        key_hot, key_order, key_other, key_local = jax.random.split(segment_key, 4)
        hot_owner = jax.random.randint(key_hot, (), 0, N_ADAPTER)
        order = jax.random.permutation(key_order, segment_rows)
        others = jax.random.permutation(key_other, N_ADAPTER - 1)
        other_owner = others[(order - OWN_MAX) % (N_ADAPTER - 1)]
        other_owner = other_owner + (other_owner >= hot_owner).astype(jnp.int32)
        owner = jnp.where(order < OWN_MAX, hot_owner, other_owner)
        local = jax.random.randint(key_local, (segment_rows,), 0, AD_DEV)
        return (owner * AD_DEV + local).astype(jnp.int32)
    segment_keys = jax.random.split(jax.random.fold_in(key, 11), N_SEGMENT)
    return jax.vmap(single_section_part)(segment_keys).reshape(-1)


def draw_cache_valid_length(key, part):
    key_len, key_pick = jax.random.split(jax.random.fold_in(key, 23))
    lengths = jax.random.randint(key_len, (ROWS,), 1, CTX + 1)
    picks = jax.random.permutation(key_pick, ROWS)
    lengths = jnp.where(picks == 0, CTX, lengths)
    lengths = jnp.where(picks == 1, 1, lengths)
    return lengths.astype(jnp.int32)


def draw_key_value_cache(key, part):
    key_keys = jax.random.fold_in(jax.random.fold_in(key, 37), 0)
    key_values = jax.random.fold_in(jax.random.fold_in(key, 37), 2)
    array_shape = (ROWS, 1, CTX, KVH * HD)
    cached_keys = jax.random.normal(key_keys, array_shape, jnp.float32)
    cached_values = jax.random.normal(key_values, array_shape, jnp.float32)
    joined = jnp.concatenate([cached_keys, cached_values], axis=1)
    return jnp.clip(joined, -1500.0, 1500.0).astype(jnp.bfloat16)


def shard_levels(rng, dims, pieces, low, top_value):
    factor_of, own = 1.0, jax.random.fold_in(rng, 6)
    for axis_at, shards_of in pieces:
        draws = jnp.exp(jax.random.uniform(jax.random.fold_in(own, axis_at), (shards_of,), jnp.float32, low / len(pieces), top_value / len(pieces)))
        factor_of = factor_of * jnp.repeat(draws, dims[axis_at] // shards_of).reshape([-1 if axis == axis_at else 1 for axis in range(len(dims))])
    return factor_of


def bell_draw(rng, shape, scale, bound, pieces=(), kind=jnp.bfloat16):
    array = jax.random.normal(rng, shape, jnp.float32) * scale
    if len(pieces) > 0:
        array = shard_levels(rng, shape, pieces, -0.22, 0.18) * array
    return jnp.clip(array, min=-bound, max=bound).astype(kind)


def setup_inputs(seed: int = 0) -> dict:
    seeds = jax.random.split(jax.random.key(seed), 9)
    return {
        "incoming": bell_draw(seeds[0], (ROWS, MODEL_WIDTH), 1.0, 6.0, ((0, 512),)),
        "attention_norm_gain": jnp.clip(1.0 + 0.18 * jax.random.normal(seeds[1], (N_SEGMENT, MODEL_WIDTH), jnp.float32), 0.1, 1.9),
        "query_weight": bell_draw(seeds[2], (N_SEGMENT, MODEL_WIDTH, MODEL_WIDTH), MODEL_WIDTH ** -0.5, 0.0625, ((0, 8), (2, 64))),
        "adapter_down_weight": bell_draw(seeds[3], (N_SEGMENT, ADAPTER_COUNT, MODEL_WIDTH, ADAPTER_RANK), MODEL_WIDTH ** -0.5, 0.0625, ((0, 8), (1, 64))),
        "adapter_up_weight": bell_draw(seeds[4], (N_SEGMENT, ADAPTER_COUNT, ADAPTER_RANK, MODEL_WIDTH), ADAPTER_RANK ** -0.5, 0.75, ((0, 8), (3, 64))),
        "request_adapter_index": draw_request_adapter_index(jax.random.fold_in(seeds[8], 71), 0),
        "cache_valid_length": draw_cache_valid_length(jax.random.fold_in(seeds[8], 71), 0),
        "key_value_cache": draw_key_value_cache(jax.random.fold_in(seeds[8], 71), 0),
    }


adapter_scale = 0.5
norm_eps = 1e-05

def reference(incoming, attention_norm_gain, query_weight, adapter_down_weight, adapter_up_weight, request_adapter_index, cache_valid_length, key_value_cache):
    segment_rows = TOK_DEV * N_ADAPTER
    received_rows = jnp.roll(incoming, segment_rows, axis=0).reshape(N_SEGMENT, segment_rows, MODEL_WIDTH)
    section_index = request_adapter_index.reshape(N_SEGMENT, segment_rows)
    section_length = cache_valid_length.reshape(N_SEGMENT, segment_rows)
    section_cache = key_value_cache.reshape(N_SEGMENT, segment_rows, 2, CTX, KVH * HD)
    group_size = HEADS // KVH

    def single_section_part(operands):
        row_block, segment_gain, weight, down_matrices, up_maps, block_index_list, block_lengths, block_cache = operands
        values = row_block.astype(jnp.float32)
        mean_square = lax.optimization_barrier(jnp.mean(values * values, axis=-1, keepdims=True))
        normalized_input = (values * lax.rsqrt(mean_square + norm_eps) * segment_gain).astype(jnp.bfloat16)
        base_query = jnp.dot(normalized_input, weight, preferred_element_type=jnp.float32)

        def single_request_row(pair_item):
            single_row, adapter = pair_item
            shrunk = jnp.dot(single_row, down_matrices[adapter], preferred_element_type=jnp.float32).astype(jnp.bfloat16)
            return jnp.dot(shrunk, up_maps[adapter], preferred_element_type=jnp.float32)
        adapter_update = lax.map(single_request_row, (normalized_input, block_index_list))
        query_rows = (base_query + adapter_scale * adapter_update).astype(jnp.bfloat16)
        query_heads = query_rows.astype(jnp.float32).reshape(segment_rows, KVH, group_size, HD)
        cached_keys = block_cache[:, 0].astype(jnp.float32).reshape(segment_rows, CTX, KVH, HD)
        cached_values = block_cache[:, 1].astype(jnp.float32).reshape(segment_rows, CTX, KVH, HD)
        scores = jnp.einsum('tkgd,tckd->tkgc', query_heads, cached_keys) * HD ** (-0.5)
        is_live = jnp.arange(CTX, dtype=jnp.int32)[None, :] < block_lengths[:, None]
        scores = jnp.where(is_live[:, None, None, :], scores, -jnp.inf)
        row_max = lax.optimization_barrier(jnp.max(scores, axis=-1, keepdims=True))
        expsum = jnp.exp(scores - row_max)
        probs = (expsum / lax.optimization_barrier(jnp.sum(expsum, axis=-1, keepdims=True))).astype(jnp.bfloat16)
        context = jnp.einsum('tkgc,tckd->tkgd', probs.astype(jnp.float32), cached_values)
        return context.astype(jnp.bfloat16).reshape(segment_rows, MODEL_WIDTH)
    output_list = lax.map(single_section_part, (received_rows, attention_norm_gain, query_weight, adapter_down_weight, adapter_up_weight, section_index, section_length, section_cache))
    return output_list.reshape(ROWS, MODEL_WIDTH)
```

```python
import jax
import jax.numpy as jnp
from jax import lax
from jax.sharding import PartitionSpec as P

MODEL_WIDTH = 8192
HEADS = 64
KVH = 8
HD = 128
CTX = 16
SIDE = 8
OWN_MAX = 32


adapter_scale = 0.5
norm_eps = 1e-05

BOTH = ("segment", "adapter")


def line_groups(segments, second):
    groups = []
    for s in range(segments):
        along_minor = (s % 2 == 0) != second
        for i in range(SIDE):
            if along_minor:
                groups.append([s * 64 + i * SIDE + j for j in range(SIDE)])
            else:
                groups.append([s * 64 + j * SIDE + i for j in range(SIDE)])
    return groups


def from_behind(value, axis, by):
    devices = lax.axis_size(axis)
    return lax.ppermute(value, axis, [(i, (i + by) % devices) for i in range(devices)])


def swap_sides(odd, value):
    shape = value.shape
    cut = value.reshape((SIDE, SIDE, -1) + shape[1:])
    return jnp.where(odd, cut.swapaxes(0, 1), cut).reshape(shape)


def body(
    incoming,
    attention_norm_gain,
    query_weight,
    adapter_down_weight,
    adapter_up_weight,
    request_adapter_index,
    cache_valid_length,
    key_value_cache,
):
    segments = lax.axis_size("segment")
    position = lax.axis_index("adapter")
    odd = lax.axis_index("segment") % 2 == 1
    received_rows = from_behind(incoming, "segment", 1)
    values = received_rows.astype(jnp.float32)
    mean_square = jnp.mean(values * values, axis=-1, keepdims=True)
    normalized_input = (values * lax.rsqrt(mean_square + norm_eps) * attention_norm_gain[0]).astype(
        jnp.bfloat16
    )
    tok_dev = received_rows.shape[0]
    segment_rows = request_adapter_index.shape[0]
    weight = query_weight[0]
    column_list = weight.shape[1]
    down = adapter_down_weight[0, 0]
    rank_width = down.shape[1]
    bank = adapter_up_weight.shape[1]

    line = lax.all_to_all(
        jnp.broadcast_to(normalized_input[None], (SIDE, tok_dev, MODEL_WIDTH)),
        BOTH,
        split_axis=0,
        concat_axis=0,
        tiled=True,
        axis_index_groups=line_groups(segments, False),
    ).reshape(SIDE * tok_dev, MODEL_WIDTH)
    rows = lax.all_gather(
        line, BOTH, axis=0, tiled=True, axis_index_groups=line_groups(segments, True)
    )

    index = swap_sides(odd, request_adapter_index)
    hot = index[:, None] == jnp.arange(bank, dtype=jnp.int32)[None, :]
    hot_counts = jnp.cumsum(hot.astype(jnp.int32), axis=0)
    slot = jnp.sum(jnp.where(hot, hot_counts, 0), axis=1) - 1
    pick = (
        (jnp.arange(OWN_MAX, dtype=jnp.int32)[:, None] == slot[None, :])
        & (index == position)[None, :]
    ).astype(jnp.bfloat16)
    place = (
        (index * OWN_MAX + slot)[:, None]
        == jnp.arange(bank * OWN_MAX, dtype=jnp.int32)[None, :]
    ).astype(jnp.bfloat16)

    shrunk_all = jnp.dot(rows, down, preferred_element_type=jnp.float32).astype(jnp.bfloat16)
    shrunk_mine = jnp.dot(pick, shrunk_all, preferred_element_type=jnp.float32).astype(jnp.bfloat16)
    flat = shrunk_mine.reshape(1, OWN_MAX * rank_width)
    shrunk_slots = lax.all_to_all(
        jnp.broadcast_to(flat, (bank, OWN_MAX * rank_width)),
        "adapter",
        split_axis=0,
        concat_axis=0,
        tiled=True,
    ).reshape(bank * OWN_MAX, rank_width)
    base_query = jnp.dot(rows, weight, preferred_element_type=jnp.float32)
    shrunk_tok = jnp.dot(place, shrunk_slots, preferred_element_type=jnp.float32).astype(
        jnp.bfloat16
    )
    spread = (hot.astype(jnp.bfloat16)[:, :, None] * shrunk_tok[:, None, :]).reshape(
        segment_rows, bank * rank_width
    )
    adapter_update = jnp.dot(
        spread,
        adapter_up_weight[0].reshape(bank * rank_width, column_list),
        preferred_element_type=jnp.float32,
    )
    query_rows = (base_query + adapter_scale * adapter_update).astype(jnp.bfloat16)
    query_rows = swap_sides(odd, query_rows)
    own_queries = lax.all_to_all(query_rows, "adapter", split_axis=0, concat_axis=1, tiled=True)
    own_lengths = lax.dynamic_slice_in_dim(cache_valid_length, position * tok_dev, tok_dev)
    group_size = HEADS // KVH
    query_heads = own_queries.reshape(tok_dev, KVH, group_size, HD)
    cached_keys = key_value_cache[:, 0].reshape(tok_dev, CTX, KVH, HD)
    cached_values = key_value_cache[:, 1].reshape(tok_dev, CTX, KVH, HD)
    scores = jnp.einsum(
        "tkgd,tckd->tkgc", query_heads, cached_keys, preferred_element_type=jnp.float32
    ) * HD ** (-0.5)
    is_live = jnp.arange(CTX, dtype=jnp.int32)[None, :] < own_lengths[:, None]
    scores = jnp.where(is_live[:, None, None, :], scores, -jnp.inf)
    row_max = jnp.max(scores, axis=-1, keepdims=True)
    expsum = jnp.exp(scores - row_max)
    probs = (expsum / jnp.sum(expsum, axis=-1, keepdims=True)).astype(jnp.bfloat16)
    context = jnp.einsum(
        "tkgc,tckd->tkgd", probs, cached_values, preferred_element_type=jnp.float32
    )
    return context.astype(jnp.bfloat16).reshape(tok_dev, MODEL_WIDTH)


def solution(mesh):
    in_specs = (
        P(("segment", "adapter"), None),
        P("segment", None),
        P("segment", None, "adapter"),
        P("segment", "adapter", None, None),
        P("segment", None, None, "adapter"),
        P("segment"),
        P("segment"),
        P(("segment", "adapter"), None, None, None),
    )
    out_specs = P(("segment", "adapter"), None)
    return jax.shard_map(body, mesh=mesh, in_specs=in_specs, out_specs=out_specs, check_vma=False)
```

```python
import jax
import jax.numpy as jnp
from jax import lax
from jax.experimental import pallas as pl
from jax.experimental.pallas import tpu as pltpu
from jax.sharding import PartitionSpec as P

MODEL_WIDTH = 8192
HEADS = 64
KVH = 8
HD = 128
CTX = 16
SIDE = 8
OWN_MAX = 32


adapter_scale = 0.5
norm_eps = 1e-05

BOTH = ("segment", "adapter")


def line_groups(segments, second):
    groups = []
    for s in range(segments):
        along_minor = (s % 2 == 0) != second
        for i in range(SIDE):
            if along_minor:
                groups.append([s * 64 + i * SIDE + j for j in range(SIDE)])
            else:
                groups.append([s * 64 + j * SIDE + i for j in range(SIDE)])
    return groups


def from_behind(value, axis, by):
    devices = lax.axis_size(axis)
    return lax.ppermute(value, axis, [(i, (i + by) % devices) for i in range(devices)])


def swap_sides(odd, value):
    shape = value.shape
    cut = value.reshape((SIDE, SIDE, -1) + shape[1:])
    return jnp.where(odd, cut.swapaxes(0, 1), cut).reshape(shape)


def over_line(blocks, groups):
    return lax.all_to_all(
        blocks, BOTH, split_axis=0, concat_axis=0, tiled=True, axis_index_groups=groups
    )


def along_line(block, groups, by):
    pairs = [(g[i], g[(i + by) % SIDE]) for g in groups for i in range(SIDE)]
    return lax.ppermute(block, BOTH, pairs)


def to_partner(block, groups):
    pairs = [(g[i], g[i ^ 1]) for g in groups for i in range(SIDE)]
    return lax.ppermute(block, BOTH, pairs)


def shrink_kernel(which_ref, mine_ref, theirs_ref, down_ref, out_ref):
    half = mine_ref.shape[1]
    shrunk = None
    for rows_ref, part in ((mine_ref, which_ref[0]), (theirs_ref, 1 - which_ref[0])):
        start = pl.multiple_of(part * half, half)
        term = lax.dot_general(
            rows_ref[...],
            down_ref[:, pl.ds(start, half)],
            (((1,), (1,)), ((), ())),
            preferred_element_type=jnp.float32,
        )
        shrunk = term if shrunk is None else shrunk + term
    some = OWN_MAX // 2
    shrunk = shrunk.astype(jnp.bfloat16)
    flat = jnp.concatenate([shrunk[:some], shrunk[some:]], axis=1)
    out_ref[...] = jnp.broadcast_to(flat[None], out_ref.shape)


def shrink(which, mine, theirs, down_t, bank):
    vmem = pl.BlockSpec(memory_space=pltpu.VMEM)
    return pl.pallas_call(
        shrink_kernel,
        out_shape=jax.ShapeDtypeStruct((bank, OWN_MAX // 2, 2 * down_t.shape[0]), jnp.bfloat16),
        in_specs=[pl.BlockSpec(memory_space=pltpu.SMEM), vmem, vmem, vmem],
        out_specs=vmem,
        compiler_params=pltpu.CompilerParams(vmem_limit_bytes=8 * 1024 * 1024),
    )(which.reshape(1), mine, theirs, down_t)


def body(
    incoming,
    attention_norm_gain,
    query_weight,
    adapter_down_weight,
    adapter_up_weight,
    request_adapter_index,
    cache_valid_length,
    key_value_cache,
):
    segments = lax.axis_size("segment")
    position = lax.axis_index("adapter")
    odd = lax.axis_index("segment") % 2 == 1
    lines_b = line_groups(segments, False)
    lines_a = line_groups(segments, True)
    minor, major = position % SIDE, position // SIDE
    at_a = jnp.where(odd, minor, major)
    at_b = jnp.where(odd, major, minor)
    which = at_b % 2
    weight = query_weight[0]
    column_list = weight.shape[1]
    down = adapter_down_weight[0, 0]
    rank_width = down.shape[1]
    bank = adapter_up_weight.shape[1]
    segment_rows = request_adapter_index.shape[0]
    half = MODEL_WIDTH // 2

    received_rows = from_behind(incoming, "segment", 1)

    weight_theirs = to_partner(
        lax.dynamic_slice_in_dim(weight, (1 - which) * half, half), lines_b
    )

    tok_dev = received_rows.shape[0]
    line_rows = SIDE * tok_dev
    values = received_rows.astype(jnp.float32)
    mean_square = jnp.mean(values * values, axis=-1, keepdims=True)
    normalized_input = (values * lax.rsqrt(mean_square + norm_eps) * attention_norm_gain[0]).astype(
        jnp.bfloat16
    )
    cut = normalized_input.reshape(tok_dev, 2, half).swapaxes(0, 1)
    line = over_line(
        jnp.broadcast_to(cut[None], (SIDE // 2, 2, tok_dev, half)).reshape(SIDE, tok_dev, half),
        lines_b,
    ).reshape(line_rows, half)

    normalized_input, weight, request_adapter_index = lax.optimization_barrier(
        (normalized_input, weight, request_adapter_index)
    )
    weight_both = lax.optimization_barrier(
        jnp.concatenate(
            [lax.dynamic_slice_in_dim(weight, which * half, half), weight_theirs], axis=1
        )
    )

    quarter = half // 2
    blocks = [None] * SIDE
    blocks[0] = ahead = behind = line
    for step in range(1, SIDE // 2):
        ahead = along_line(ahead, lines_a, 1)
        behind = along_line(behind, lines_a, -1)
        blocks[SIDE - step], blocks[step] = ahead, behind
    far_low = along_line(ahead[:, :quarter], lines_a, 1)
    far_high = along_line(behind[:, quarter:], lines_a, -1)

    adapters = jnp.arange(bank, dtype=jnp.int32)[None, :]
    named = request_adapter_index[:, None] == adapters
    counts = jnp.cumsum(named.astype(jnp.int32), axis=0)
    slot = jnp.sum(jnp.where(named, counts, 0), axis=1) - 1
    both = jnp.stack([request_adapter_index, slot], axis=1)
    both = swap_sides(odd, both).reshape(SIDE, line_rows, 2)
    both = jnp.roll(both, -at_a, axis=0).reshape(segment_rows, 2)
    index, slot = both[:, 0], both[:, 1]
    hot = index[:, None] == adapters
    partner = jnp.where(odd, position + SIDE * (1 - 2 * which), position + (1 - 2 * which))
    owners = jnp.stack([position, partner])
    pick = (
        (jnp.arange(OWN_MAX, dtype=jnp.int32)[None, :, None] == slot[None, None, :])
        & (index[None, None, :] == owners[:, None, None])
    ).astype(jnp.bfloat16).reshape(2 * OWN_MAX, SIDE, line_rows)
    some = OWN_MAX // 2
    place = (
        (index * some + slot % some)[:, None]
        == jnp.arange(bank * some, dtype=jnp.int32)[None, :]
    ).astype(jnp.bfloat16)

    def pick_from(j, block):
        return jnp.dot(pick[:, j], block, preferred_element_type=jnp.float32).astype(jnp.bfloat16)

    picked = pick_from(0, line)
    for step in range(1, SIDE // 2):
        for j in (SIDE - step, step):
            picked = picked + pick_from(j, blocks[j])
    far = SIDE // 2
    picked = picked + jnp.concatenate(
        [pick_from(far, far_low), pick_from(far, far_high)], axis=1
    )
    picked_theirs = to_partner(picked[OWN_MAX:], lines_b)
    shrunk = shrink(which, picked[:OWN_MAX], picked_theirs, down.T, bank)
    def times(block, low=0, high=half):
        return jnp.dot(block, weight_both[low:high], preferred_element_type=jnp.float32)

    products = [None if block is None else times(block) for block in blocks]
    products[far] = times(far_low, 0, quarter) + times(far_high, quarter, half)
    product = jnp.concatenate(products, axis=0)
    shrunk, product = lax.optimization_barrier((shrunk, product))
    slots = lax.all_to_all(
        shrunk,
        "adapter",
        split_axis=0,
        concat_axis=0,
        tiled=True,
    ).reshape(bank * some, 2 * rank_width)

    base_query = product[:, :column_list] + to_partner(product[:, column_list:], lines_b)
    both = jnp.dot(place, slots, preferred_element_type=jnp.float32).astype(jnp.bfloat16)
    shrunk_tok = jnp.where((slot < some)[:, None], both[:, :rank_width], both[:, rank_width:])
    spread = (hot.astype(jnp.bfloat16)[:, :, None] * shrunk_tok[:, None, :]).reshape(
        segment_rows, bank * rank_width
    )
    adapter_update = jnp.dot(
        spread,
        adapter_up_weight[0].reshape(bank * rank_width, column_list),
        preferred_element_type=jnp.float32,
    )
    query_rows = (base_query + adapter_scale * adapter_update).astype(jnp.bfloat16)
    query_rows = query_rows.reshape(SIDE, line_rows, column_list)
    query_rows = jnp.roll(query_rows, at_a, axis=0)
    query_rows = swap_sides(odd, query_rows.reshape(segment_rows, column_list))
    own_queries = lax.all_to_all(
        query_rows.reshape(HEADS, tok_dev, HD), "adapter", split_axis=0, concat_axis=0, tiled=True
    )
    own_lengths = lax.dynamic_slice_in_dim(cache_valid_length, position * tok_dev, tok_dev)
    group_size = HEADS // KVH
    query_heads = own_queries.reshape(KVH, group_size, tok_dev, HD)
    cached_keys = key_value_cache[:, 0].reshape(tok_dev, CTX, KVH, HD)
    cached_values = key_value_cache[:, 1].reshape(tok_dev, CTX, KVH, HD)
    scores = jnp.einsum(
        "kgtd,tckd->tkgc", query_heads, cached_keys, preferred_element_type=jnp.float32
    ) * HD ** (-0.5)
    is_live = jnp.arange(CTX, dtype=jnp.int32)[None, :] < own_lengths[:, None]
    scores = jnp.where(is_live[:, None, None, :], scores, -jnp.inf)
    row_max = jnp.max(scores, axis=-1, keepdims=True)
    expsum = jnp.exp(scores - row_max)
    probs = (expsum / jnp.sum(expsum, axis=-1, keepdims=True)).astype(jnp.bfloat16)
    context = jnp.einsum(
        "tkgc,tckd->tkgd", probs, cached_values, preferred_element_type=jnp.float32
    )
    return context.astype(jnp.bfloat16).reshape(tok_dev, MODEL_WIDTH)


def solution(mesh):
    in_specs = (
        P(("segment", "adapter"), None),
        P("segment", None),
        P("segment", None, "adapter"),
        P("segment", "adapter", None, None),
        P("segment", None, None, "adapter"),
        P("segment"),
        P("segment"),
        P(("segment", "adapter"), None, None, None),
    )
    out_specs = P(("segment", "adapter"), None)
    return jax.shard_map(body, mesh=mesh, in_specs=in_specs, out_specs=out_specs, check_vma=False)
```

```python
import jax
import jax.numpy as jnp
from jax import lax
from jax.experimental import pallas as pl
from jax.experimental.pallas import tpu as pltpu
from jax.sharding import PartitionSpec as P

MODEL_WIDTH = 8192
HEADS = 64
KVH = 8
HD = 128
CTX = 16
SIDE = 8
OWN_MAX = 32


adapter_scale = 0.5
norm_eps = 1e-05

BOTH = ("segment", "adapter")


def line_groups(segments, second):
    groups = []
    for s in range(segments):
        along_minor = (s % 2 == 0) != second
        for i in range(SIDE):
            if along_minor:
                groups.append([s * 64 + i * SIDE + j for j in range(SIDE)])
            else:
                groups.append([s * 64 + j * SIDE + i for j in range(SIDE)])
    return groups


def from_behind(value, axis, by):
    devices = lax.axis_size(axis)
    return lax.ppermute(value, axis, [(i, (i + by) % devices) for i in range(devices)])


def swap_sides(odd, value):
    shape = value.shape
    cut = value.reshape((SIDE, SIDE, -1) + shape[1:])
    return jnp.where(odd, cut.swapaxes(0, 1), cut).reshape(shape)


def over_line(blocks, groups):
    return lax.all_to_all(
        blocks, BOTH, split_axis=0, concat_axis=0, tiled=True, axis_index_groups=groups
    )


def along_line(block, groups, by):
    pairs = [(g[i], g[(i + by) % SIDE]) for g in groups for i in range(SIDE)]
    return lax.ppermute(block, BOTH, pairs)


def to_partner(block, groups):
    pairs = [(g[i], g[i ^ 1]) for g in groups for i in range(SIDE)]
    return lax.ppermute(block, BOTH, pairs)


def shrink_kernel(which_ref, mine_ref, theirs_ref, down_ref, out_ref):
    half = mine_ref.shape[1]
    shrunk = None
    for rows_ref, part in ((mine_ref, which_ref[0]), (theirs_ref, 1 - which_ref[0])):
        start = pl.multiple_of(part * half, half)
        term = lax.dot_general(
            rows_ref[...],
            down_ref[:, pl.ds(start, half)],
            (((1,), (1,)), ((), ())),
            preferred_element_type=jnp.float32,
        )
        shrunk = term if shrunk is None else shrunk + term
    some = OWN_MAX // 2
    shrunk = shrunk.astype(jnp.bfloat16)
    flat = jnp.concatenate([shrunk[:some], shrunk[some:]], axis=1)
    out_ref[...] = jnp.broadcast_to(flat[None], out_ref.shape)


def shrink(which, mine, theirs, down_t, bank):
    vmem = pl.BlockSpec(memory_space=pltpu.VMEM)
    return pl.pallas_call(
        shrink_kernel,
        out_shape=jax.ShapeDtypeStruct((bank, OWN_MAX // 2, 2 * down_t.shape[0]), jnp.bfloat16),
        in_specs=[pl.BlockSpec(memory_space=pltpu.SMEM), vmem, vmem, vmem],
        out_specs=vmem,
        compiler_params=pltpu.CompilerParams(vmem_limit_bytes=8 * 1024 * 1024),
    )(which.reshape(1), mine, theirs, down_t)


def body(
    incoming,
    attention_norm_gain,
    query_weight,
    adapter_down_weight,
    adapter_up_weight,
    request_adapter_index,
    cache_valid_length,
    key_value_cache,
):
    segments = lax.axis_size("segment")
    position = lax.axis_index("adapter")
    odd = lax.axis_index("segment") % 2 == 1
    lines_b = line_groups(segments, False)
    lines_a = line_groups(segments, True)
    minor, major = position % SIDE, position // SIDE
    at_a = jnp.where(odd, minor, major)
    at_b = jnp.where(odd, major, minor)
    which = at_b % 2
    weight = query_weight[0]
    column_list = weight.shape[1]
    down = adapter_down_weight[0, 0]
    rank_width = down.shape[1]
    bank = adapter_up_weight.shape[1]
    segment_rows = request_adapter_index.shape[0]
    half = MODEL_WIDTH // 2

    received_rows = from_behind(incoming, "segment", 1)

    weight_theirs = to_partner(
        lax.dynamic_slice_in_dim(weight, (1 - which) * half, half), lines_b
    )

    tok_dev = received_rows.shape[0]
    line_rows = SIDE * tok_dev
    values = received_rows.astype(jnp.float32)
    mean_square = jnp.mean(values * values, axis=-1, keepdims=True)
    normalized_input = (values * lax.rsqrt(mean_square + norm_eps) * attention_norm_gain[0]).astype(
        jnp.bfloat16
    )
    cut = normalized_input.reshape(tok_dev, 2, half).swapaxes(0, 1)
    line = over_line(
        jnp.broadcast_to(cut[None], (SIDE // 2, 2, tok_dev, half)).reshape(SIDE, tok_dev, half),
        lines_b,
    ).reshape(line_rows, half)

    normalized_input, weight, request_adapter_index = lax.optimization_barrier(
        (normalized_input, weight, request_adapter_index)
    )
    weight_both = lax.optimization_barrier(
        jnp.concatenate(
            [lax.dynamic_slice_in_dim(weight, which * half, half), weight_theirs], axis=1
        )
    )

    quarter = half // 2
    blocks = [None] * SIDE
    blocks[0] = ahead = behind = line
    for step in range(1, SIDE // 2):
        if step == 3:
            low_piece, high_piece = ahead[:, :quarter], behind[:, quarter:]
        ahead = along_line(ahead, lines_a, 1)
        behind = along_line(behind, lines_a, -1)
        blocks[SIDE - step], blocks[step] = ahead, behind
    far_low = along_line(low_piece, lines_a, 2)
    far_high = along_line(high_piece, lines_a, -2)

    adapters = jnp.arange(bank, dtype=jnp.int32)[None, :]
    named = request_adapter_index[:, None] == adapters
    counts = jnp.cumsum(named.astype(jnp.int32), axis=0)
    slot = jnp.sum(jnp.where(named, counts, 0), axis=1) - 1
    some = OWN_MAX // 2
    place = (
        (request_adapter_index * some + slot % some)[:, None]
        == jnp.arange(bank * some, dtype=jnp.int32)[None, :]
    ).astype(jnp.bfloat16)
    lower = (slot < some)[:, None]
    turned = jnp.stack([request_adapter_index, slot], axis=1)
    turned = swap_sides(odd, turned).reshape(SIDE, line_rows, 2)
    turned = jnp.roll(turned, -at_a, axis=0).reshape(segment_rows, 2)
    index, turned_slot = turned[:, 0], turned[:, 1]
    partner = jnp.where(odd, position + SIDE * (1 - 2 * which), position + (1 - 2 * which))
    owners = jnp.stack([position, partner])
    pick = (
        (jnp.arange(OWN_MAX, dtype=jnp.int32)[None, :, None] == turned_slot[None, None, :])
        & (index[None, None, :] == owners[:, None, None])
    ).astype(jnp.bfloat16).reshape(2 * OWN_MAX, SIDE, line_rows)
    def pick_from(j, block):
        return jnp.dot(pick[:, j], block, preferred_element_type=jnp.float32).astype(jnp.bfloat16)

    picked = pick_from(0, line)
    for step in range(1, SIDE // 2):
        for j in (SIDE - step, step):
            picked = picked + pick_from(j, blocks[j])
    far = SIDE // 2
    picked = picked + jnp.concatenate(
        [pick_from(far, far_low), pick_from(far, far_high)], axis=1
    )
    picked_theirs = to_partner(picked[OWN_MAX:], lines_b)
    shrunk = shrink(which, picked[:OWN_MAX], picked_theirs, down.T, bank)
    def times(block, low=0, high=half):
        return jnp.dot(block, weight_both[low:high], preferred_element_type=jnp.float32)

    products = [None if block is None else times(block) for block in blocks]
    products[far] = times(far_low, 0, quarter) + times(far_high, quarter, half)
    product = jnp.concatenate(products, axis=0)
    shrunk, product = lax.optimization_barrier((shrunk, product))
    product = jnp.roll(product.reshape(SIDE, line_rows, -1), at_a, axis=0)
    product = swap_sides(odd, product.reshape(segment_rows, -1))
    slots = lax.all_to_all(
        shrunk,
        "adapter",
        split_axis=0,
        concat_axis=0,
        tiled=True,
    ).reshape(bank * some, 2 * rank_width)

    base_query = product[:, :column_list] + to_partner(product[:, column_list:], lines_b)
    both = jnp.dot(place, slots, preferred_element_type=jnp.float32).astype(jnp.bfloat16)
    shrunk_tok = jnp.where(lower, both[:, :rank_width], both[:, rank_width:])
    spread = (named.astype(jnp.bfloat16)[:, :, None] * shrunk_tok[:, None, :]).reshape(
        segment_rows, bank * rank_width
    )
    adapter_update = jnp.dot(
        spread,
        adapter_up_weight[0].reshape(bank * rank_width, column_list),
        preferred_element_type=jnp.float32,
    )
    query_rows = (base_query + adapter_scale * adapter_update).astype(jnp.bfloat16)
    own_queries = lax.all_to_all(
        query_rows.reshape(HEADS, tok_dev, HD), "adapter", split_axis=0, concat_axis=0, tiled=True
    )
    own_lengths = lax.dynamic_slice_in_dim(cache_valid_length, position * tok_dev, tok_dev)
    group_size = HEADS // KVH
    query_heads = own_queries.reshape(KVH, group_size, tok_dev, HD)
    cached_keys = key_value_cache[:, 0].reshape(tok_dev, CTX, KVH, HD)
    cached_values = key_value_cache[:, 1].reshape(tok_dev, CTX, KVH, HD)
    scores = jnp.einsum(
        "kgtd,tckd->tkgc", query_heads, cached_keys, preferred_element_type=jnp.float32
    ) * HD ** (-0.5)
    is_live = jnp.arange(CTX, dtype=jnp.int32)[None, :] < own_lengths[:, None]
    scores = jnp.where(is_live[:, None, None, :], scores, -jnp.inf)
    row_max = jnp.max(scores, axis=-1, keepdims=True)
    expsum = jnp.exp(scores - row_max)
    probs = (expsum / jnp.sum(expsum, axis=-1, keepdims=True)).astype(jnp.bfloat16)
    context = jnp.einsum(
        "tkgc,tckd->tkgd", probs, cached_values, preferred_element_type=jnp.float32
    )
    return context.astype(jnp.bfloat16).reshape(tok_dev, MODEL_WIDTH)


def solution(mesh):
    in_specs = (
        P(("segment", "adapter"), None),
        P("segment", None),
        P("segment", None, "adapter"),
        P("segment", "adapter", None, None),
        P("segment", None, None, "adapter"),
        P("segment"),
        P("segment"),
        P(("segment", "adapter"), None, None, None),
    )
    out_specs = P(("segment", "adapter"), None)
    return jax.shard_map(body, mesh=mesh, in_specs=in_specs, out_specs=out_specs, check_vma=False)
```

```python
import jax
import jax.numpy as jnp
from jax import lax
from jax.experimental import pallas as pl
from jax.experimental.pallas import tpu as pltpu
from jax.sharding import PartitionSpec as P

MODEL_WIDTH = 8192
HEADS = 64
KVH = 8
HD = 128
CTX = 16
SIDE = 8
OWN_MAX = 32


adapter_scale = 0.5
norm_eps = 1e-05

BOTH = ("segment", "adapter")


def line_groups(segments, second):
    groups = []
    for s in range(segments):
        along_minor = (s % 2 == 0) != second
        for i in range(SIDE):
            if along_minor:
                groups.append([s * 64 + i * SIDE + j for j in range(SIDE)])
            else:
                groups.append([s * 64 + j * SIDE + i for j in range(SIDE)])
    return groups


def from_behind(value, axis, by):
    devices = lax.axis_size(axis)
    return lax.ppermute(value, axis, [(i, (i + by) % devices) for i in range(devices)])


def swap_sides(odd, value):
    shape = value.shape
    cut = value.reshape((SIDE, SIDE, -1) + shape[1:])
    return jnp.where(odd, cut.swapaxes(0, 1), cut).reshape(shape)


def over_line(blocks, groups):
    return lax.all_to_all(
        blocks, BOTH, split_axis=0, concat_axis=0, tiled=True, axis_index_groups=groups
    )


def along_line(block, groups, by):
    pairs = [(g[i], g[(i + by) % SIDE]) for g in groups for i in range(SIDE)]
    return lax.ppermute(block, BOTH, pairs)


def to_partner(block, groups):
    pairs = [(g[i], g[i ^ 1]) for g in groups for i in range(SIDE)]
    return lax.ppermute(block, BOTH, pairs)


def shrink_kernel(which_ref, mine_ref, theirs_ref, down_ref, out_ref):
    half = mine_ref.shape[1]
    shrunk = None
    for rows_ref, part in ((mine_ref, which_ref[0]), (theirs_ref, 1 - which_ref[0])):
        start = pl.multiple_of(part * half, half)
        term = lax.dot_general(
            rows_ref[...],
            down_ref[:, pl.ds(start, half)],
            (((1,), (1,)), ((), ())),
            preferred_element_type=jnp.float32,
        )
        shrunk = term if shrunk is None else shrunk + term
    some = OWN_MAX // 2
    shrunk = shrunk.astype(jnp.bfloat16)
    flat = jnp.concatenate([shrunk[:some], shrunk[some:]], axis=1)
    out_ref[...] = jnp.broadcast_to(flat[None], out_ref.shape)


def shrink(which, mine, theirs, down_t, bank):
    vmem = pl.BlockSpec(memory_space=pltpu.VMEM)
    return pl.pallas_call(
        shrink_kernel,
        out_shape=jax.ShapeDtypeStruct((bank, OWN_MAX // 2, 2 * down_t.shape[0]), jnp.bfloat16),
        in_specs=[pl.BlockSpec(memory_space=pltpu.SMEM), vmem, vmem, vmem],
        out_specs=vmem,
        compiler_params=pltpu.CompilerParams(vmem_limit_bytes=8 * 1024 * 1024),
    )(which.reshape(1), mine, theirs, down_t)


def body(
    incoming,
    attention_norm_gain,
    query_weight,
    adapter_down_weight,
    adapter_up_weight,
    request_adapter_index,
    cache_valid_length,
    key_value_cache,
):
    segments = lax.axis_size("segment")
    position = lax.axis_index("adapter")
    odd = lax.axis_index("segment") % 2 == 1
    lines_b = line_groups(segments, False)
    lines_a = line_groups(segments, True)
    minor, major = position % SIDE, position // SIDE
    at_a = jnp.where(odd, minor, major)
    at_b = jnp.where(odd, major, minor)
    which = at_b % 2
    weight = query_weight[0]
    column_list = weight.shape[1]
    down = adapter_down_weight[0, 0]
    rank_width = down.shape[1]
    bank = adapter_up_weight.shape[1]
    segment_rows = request_adapter_index.shape[0]
    half = MODEL_WIDTH // 2

    received_rows = from_behind(incoming, "segment", 1)

    weight_theirs = to_partner(
        lax.dynamic_slice_in_dim(weight, (1 - which) * half, half), lines_b
    )

    tok_dev = received_rows.shape[0]
    line_rows = SIDE * tok_dev
    values = received_rows.astype(jnp.float32)
    mean_square = jnp.mean(values * values, axis=-1, keepdims=True)
    normalized_input = (values * lax.rsqrt(mean_square + norm_eps) * attention_norm_gain[0]).astype(
        jnp.bfloat16
    )
    cut = normalized_input.reshape(tok_dev, 2, half).swapaxes(0, 1)
    line = over_line(
        jnp.broadcast_to(cut[None], (SIDE // 2, 2, tok_dev, half)).reshape(SIDE, tok_dev, half),
        lines_b,
    ).reshape(line_rows, half)

    normalized_input, weight, request_adapter_index = lax.optimization_barrier(
        (normalized_input, weight, request_adapter_index)
    )
    weight_both = lax.optimization_barrier(
        jnp.concatenate(
            [lax.dynamic_slice_in_dim(weight, which * half, half), weight_theirs], axis=1
        )
    )

    quarter = half // 2
    blocks = [None] * SIDE
    blocks[0] = ahead = behind = line
    for step in range(1, SIDE // 2):
        if step == 3:
            low_piece, high_piece = ahead[:, :quarter], behind[:, quarter:]
        ahead = along_line(ahead, lines_a, 1)
        behind = along_line(behind, lines_a, -1)
        blocks[SIDE - step], blocks[step] = ahead, behind
    far_low = along_line(low_piece, lines_a, 2)
    far_high = along_line(high_piece, lines_a, -2)

    adapters = jnp.arange(bank, dtype=jnp.int32)[None, :]
    named = request_adapter_index[:, None] == adapters
    counts = jnp.cumsum(named.astype(jnp.int32), axis=0)
    slot = jnp.sum(jnp.where(named, counts, 0), axis=1) - 1
    some = OWN_MAX // 2
    place = (
        (request_adapter_index * some + slot % some)[:, None]
        == jnp.arange(bank * some, dtype=jnp.int32)[None, :]
    ).astype(jnp.bfloat16)
    lower = (slot < some)[:, None]
    turned = jnp.stack([request_adapter_index, slot], axis=1)
    turned = swap_sides(odd, turned).reshape(SIDE, line_rows, 2)
    turned = jnp.roll(turned, -at_a, axis=0).reshape(segment_rows, 2)
    index, turned_slot = turned[:, 0], turned[:, 1]
    partner = jnp.where(odd, position + SIDE * (1 - 2 * which), position + (1 - 2 * which))
    owners = jnp.stack([position, partner])
    pick = (
        (jnp.arange(OWN_MAX, dtype=jnp.int32)[None, :, None] == turned_slot[None, None, :])
        & (index[None, None, :] == owners[:, None, None])
    ).astype(jnp.bfloat16).reshape(2 * OWN_MAX, SIDE, line_rows)
    def pick_from(j, block):
        return jnp.dot(pick[:, j], block, preferred_element_type=jnp.float32).astype(jnp.bfloat16)

    picked = pick_from(0, line)
    for step in range(1, SIDE // 2):
        for j in (SIDE - step, step):
            picked = picked + pick_from(j, blocks[j])
    far = SIDE // 2
    picked = picked + jnp.concatenate(
        [pick_from(far, far_low), pick_from(far, far_high)], axis=1
    )
    picked_theirs = to_partner(picked[OWN_MAX:], lines_b)
    shrunk = shrink(which, picked[:OWN_MAX], picked_theirs, down.T, bank)
    def times(block, low=0, high=half):
        return jnp.dot(block, weight_both[low:high], preferred_element_type=jnp.float32)

    products = [None if block is None else times(block) for block in blocks]
    products[far] = times(far_low, 0, quarter) + times(far_high, quarter, half)
    product = jnp.concatenate(products, axis=0)
    shrunk, product = lax.optimization_barrier((shrunk, product))
    product = jnp.roll(product.reshape(SIDE, line_rows, -1), at_a, axis=0)
    product = swap_sides(odd, product.reshape(segment_rows, -1))
    slots = lax.all_to_all(
        shrunk,
        "adapter",
        split_axis=0,
        concat_axis=0,
        tiled=True,
    ).reshape(bank * some, 2 * rank_width)

    base_query = product[:, :column_list] + to_partner(product[:, column_list:], lines_b)
    both = jnp.dot(place, slots, preferred_element_type=jnp.float32).astype(jnp.bfloat16)
    shrunk_tok = jnp.where(lower, both[:, :rank_width], both[:, rank_width:])
    spread = (named.astype(jnp.bfloat16)[:, :, None] * shrunk_tok[:, None, :]).reshape(
        segment_rows, bank * rank_width
    )
    adapter_update = jnp.dot(
        spread,
        adapter_up_weight[0].reshape(bank * rank_width, column_list),
        preferred_element_type=jnp.float32,
    )
    query_rows = (base_query + adapter_scale * adapter_update).astype(jnp.bfloat16)
    own_queries = lax.all_to_all(
        query_rows.reshape(HEADS, tok_dev, HD), "adapter", split_axis=0, concat_axis=0, tiled=True
    )
    own_lengths = lax.dynamic_slice_in_dim(cache_valid_length, position * tok_dev, tok_dev)
    group_size = HEADS // KVH
    queries = own_queries.reshape(KVH, group_size * tok_dev, HD)
    cache = key_value_cache.reshape(tok_dev, 2, CTX, KVH, HD).transpose(1, 3, 0, 2, 4)
    cached_keys = cache[0].reshape(KVH, tok_dev * CTX, HD)
    cached_values = cache[1].reshape(KVH, tok_dev * CTX, HD)
    row_token = jnp.arange(group_size * tok_dev, dtype=jnp.int32)[:, None] % tok_dev
    column = jnp.arange(tok_dev * CTX, dtype=jnp.int32)[None, :]
    live = jnp.tile(own_lengths, group_size)[:, None]
    seen = (column // CTX == row_token) & (column % CTX < live)
    scores = jnp.einsum(
        "krd,kcd->krc", queries, cached_keys, preferred_element_type=jnp.float32
    ) * HD ** (-0.5)
    scores = jnp.where(seen[None], scores, -jnp.inf)
    row_max = jnp.max(scores, axis=-1, keepdims=True)
    expsum = jnp.exp(scores - row_max)
    probs = (expsum / jnp.sum(expsum, axis=-1, keepdims=True)).astype(jnp.bfloat16)
    context = jnp.einsum("krc,kcd->krd", probs, cached_values, preferred_element_type=jnp.float32)
    context = context.astype(jnp.bfloat16).reshape(HEADS, tok_dev, HD)
    return context.transpose(1, 0, 2).reshape(tok_dev, MODEL_WIDTH)


def solution(mesh):
    in_specs = (
        P(("segment", "adapter"), None),
        P("segment", None),
        P("segment", None, "adapter"),
        P("segment", "adapter", None, None),
        P("segment", None, None, "adapter"),
        P("segment"),
        P("segment"),
        P(("segment", "adapter"), None, None, None),
    )
    out_specs = P(("segment", "adapter"), None)
    return jax.shard_map(body, mesh=mesh, in_specs=in_specs, out_specs=out_specs, check_vma=False)
```

```python
import jax
import jax.numpy as jnp
from jax import lax
from jax.experimental import pallas as pl
from jax.experimental.pallas import tpu as pltpu
from jax.sharding import PartitionSpec as P

MODEL_WIDTH = 8192
HEADS = 64
KVH = 8
HD = 128
CTX = 16
SIDE = 8
OWN_MAX = 32


adapter_scale = 0.5
norm_eps = 1e-05

BOTH = ("segment", "adapter")


def line_groups(segments, second):
    groups = []
    for s in range(segments):
        along_minor = (s % 2 == 0) != second
        for i in range(SIDE):
            if along_minor:
                groups.append([s * 64 + i * SIDE + j for j in range(SIDE)])
            else:
                groups.append([s * 64 + j * SIDE + i for j in range(SIDE)])
    return groups


def from_behind(value, axis, by):
    devices = lax.axis_size(axis)
    return lax.ppermute(value, axis, [(i, (i + by) % devices) for i in range(devices)])


def swap_sides(odd, value):
    shape = value.shape
    cut = value.reshape((SIDE, SIDE, -1) + shape[1:])
    return jnp.where(odd, cut.swapaxes(0, 1), cut).reshape(shape)


def over_line(blocks, groups):
    return lax.all_to_all(
        blocks, BOTH, split_axis=0, concat_axis=0, tiled=True, axis_index_groups=groups
    )


def along_line(block, groups, by):
    pairs = [(g[i], g[(i + by) % SIDE]) for g in groups for i in range(SIDE)]
    return lax.ppermute(block, BOTH, pairs)


def to_partner(block, groups):
    pairs = [(g[i], g[i ^ 1]) for g in groups for i in range(SIDE)]
    return lax.ppermute(block, BOTH, pairs)


def shrink_kernel(which_ref, mine_ref, theirs_ref, down_ref, out_ref):
    half = mine_ref.shape[1]
    shrunk = None
    for rows_ref, part in ((mine_ref, which_ref[0]), (theirs_ref, 1 - which_ref[0])):
        start = pl.multiple_of(part * half, half)
        term = lax.dot_general(
            rows_ref[...],
            down_ref[:, pl.ds(start, half)],
            (((1,), (1,)), ((), ())),
            preferred_element_type=jnp.float32,
        )
        shrunk = term if shrunk is None else shrunk + term
    some = OWN_MAX // 2
    shrunk = shrunk.astype(jnp.bfloat16)
    flat = jnp.concatenate([shrunk[:some], shrunk[some:]], axis=1)
    out_ref[...] = jnp.broadcast_to(flat[None], out_ref.shape)


def shrink(which, mine, theirs, down_t, bank):
    vmem = pl.BlockSpec(memory_space=pltpu.VMEM)
    return pl.pallas_call(
        shrink_kernel,
        out_shape=jax.ShapeDtypeStruct((bank, OWN_MAX // 2, 2 * down_t.shape[0]), jnp.bfloat16),
        in_specs=[pl.BlockSpec(memory_space=pltpu.SMEM), vmem, vmem, vmem],
        out_specs=vmem,
        compiler_params=pltpu.CompilerParams(vmem_limit_bytes=8 * 1024 * 1024),
    )(which.reshape(1), mine, theirs, down_t)


def body(
    incoming,
    attention_norm_gain,
    query_weight,
    adapter_down_weight,
    adapter_up_weight,
    request_adapter_index,
    cache_valid_length,
    key_value_cache,
):
    segments = lax.axis_size("segment")
    position = lax.axis_index("adapter")
    odd = lax.axis_index("segment") % 2 == 1
    lines_b = line_groups(segments, False)
    lines_a = line_groups(segments, True)
    minor, major = position % SIDE, position // SIDE
    at_a = jnp.where(odd, minor, major)
    at_b = jnp.where(odd, major, minor)
    which = at_b % 2
    weight = query_weight[0]
    column_list = weight.shape[1]
    down = adapter_down_weight[0, 0]
    rank_width = down.shape[1]
    bank = adapter_up_weight.shape[1]
    segment_rows = request_adapter_index.shape[0]
    half = MODEL_WIDTH // 2

    received_rows = from_behind(incoming, "segment", 1)

    weight_theirs = to_partner(
        lax.dynamic_slice_in_dim(weight, (1 - which) * half, half), lines_b
    )

    tok_dev = received_rows.shape[0]
    line_rows = SIDE * tok_dev
    values = received_rows.astype(jnp.float32)
    mean_square = jnp.mean(values * values, axis=-1, keepdims=True)
    normalized_input = (values * lax.rsqrt(mean_square + norm_eps) * attention_norm_gain[0]).astype(
        jnp.bfloat16
    )
    cut = normalized_input.reshape(tok_dev, 2, half).swapaxes(0, 1)
    line = over_line(
        jnp.broadcast_to(cut[None], (SIDE // 2, 2, tok_dev, half)).reshape(SIDE, tok_dev, half),
        lines_b,
    ).reshape(line_rows, half)

    normalized_input, weight, request_adapter_index = lax.optimization_barrier(
        (normalized_input, weight, request_adapter_index)
    )
    weight_both = lax.optimization_barrier(
        jnp.concatenate(
            [lax.dynamic_slice_in_dim(weight, which * half, half), weight_theirs], axis=1
        )
    )

    quarter = half // 2
    blocks = [None] * SIDE
    blocks[0] = ahead = behind = line
    for step in range(1, SIDE // 2):
        if step == 3:
            low_piece, high_piece = ahead[:, :quarter], behind[:, quarter:]
        ahead = along_line(ahead, lines_a, 1)
        behind = along_line(behind, lines_a, -1)
        blocks[SIDE - step], blocks[step] = ahead, behind
    far_low = along_line(low_piece, lines_a, 2)
    far_high = along_line(high_piece, lines_a, -2)

    adapters = jnp.arange(bank, dtype=jnp.int32)[None, :]
    named = request_adapter_index[:, None] == adapters
    counts = jnp.cumsum(named.astype(jnp.int32), axis=0)
    slot = jnp.sum(jnp.where(named, counts, 0), axis=1) - 1
    some = OWN_MAX // 2
    place = (
        (request_adapter_index * some + slot % some)[:, None]
        == jnp.arange(bank * some, dtype=jnp.int32)[None, :]
    ).astype(jnp.bfloat16)
    lower = (slot < some)[:, None]
    turned = jnp.stack([request_adapter_index, slot], axis=1)
    turned = swap_sides(odd, turned).reshape(SIDE, line_rows, 2)
    turned = jnp.roll(turned, -at_a, axis=0).reshape(segment_rows, 2)
    index, turned_slot = turned[:, 0], turned[:, 1]
    partner = jnp.where(odd, position + SIDE * (1 - 2 * which), position + (1 - 2 * which))
    owners = jnp.stack([position, partner])
    pick = (
        (jnp.arange(OWN_MAX, dtype=jnp.int32)[None, :, None] == turned_slot[None, None, :])
        & (index[None, None, :] == owners[:, None, None])
    ).astype(jnp.bfloat16).reshape(2 * OWN_MAX, SIDE, line_rows)
    def pick_from(j, block):
        return jnp.dot(pick[:, j], block, preferred_element_type=jnp.float32).astype(jnp.bfloat16)

    picked = pick_from(0, line)
    for step in range(1, SIDE // 2):
        for j in (SIDE - step, step):
            picked = picked + pick_from(j, blocks[j])
    far = SIDE // 2
    picked = picked + jnp.concatenate(
        [pick_from(far, far_low), pick_from(far, far_high)], axis=1
    )
    picked_theirs = to_partner(picked[OWN_MAX:], lines_b)
    shrunk = shrink(which, picked[:OWN_MAX], picked_theirs, down.T, bank)
    def times(block, low=0, high=half):
        return jnp.dot(block, weight_both[low:high], preferred_element_type=jnp.float32)

    products = [None if block is None else times(block) for block in blocks]
    products[far] = times(far_low, 0, quarter) + times(far_high, quarter, half)
    product = jnp.concatenate(products, axis=0)
    shrunk, product = lax.optimization_barrier((shrunk, product))

    def in_order(part):
        part = jnp.roll(part.reshape(SIDE, line_rows, column_list), at_a, axis=0)
        return swap_sides(odd, part.reshape(segment_rows, column_list))

    slots = lax.all_to_all(
        shrunk,
        "adapter",
        split_axis=0,
        concat_axis=0,
        tiled=True,
    ).reshape(bank * some, 2 * rank_width)

    base_query = in_order(product[:, :column_list]) + to_partner(
        in_order(product[:, column_list:]), lines_b
    )
    both = jnp.dot(place, slots, preferred_element_type=jnp.float32).astype(jnp.bfloat16)
    shrunk_tok = jnp.where(lower, both[:, :rank_width], both[:, rank_width:])
    spread = (named.astype(jnp.bfloat16)[:, :, None] * shrunk_tok[:, None, :]).reshape(
        segment_rows, bank * rank_width
    )
    adapter_update = jnp.dot(
        spread,
        adapter_up_weight[0].reshape(bank * rank_width, column_list),
        preferred_element_type=jnp.float32,
    )
    query_rows = (base_query + adapter_scale * adapter_update).astype(jnp.bfloat16)
    own_queries = lax.all_to_all(
        query_rows.reshape(HEADS, tok_dev, HD), "adapter", split_axis=0, concat_axis=0, tiled=True
    )
    own_lengths = lax.dynamic_slice_in_dim(cache_valid_length, position * tok_dev, tok_dev)
    group_size = HEADS // KVH
    query_heads = own_queries.reshape(KVH, group_size, tok_dev, HD)
    cached_keys = key_value_cache[:, 0].reshape(tok_dev, CTX, KVH, HD)
    cached_values = key_value_cache[:, 1].reshape(tok_dev, CTX, KVH, HD)
    scores = jnp.einsum(
        "kgtd,tckd->tkgc", query_heads, cached_keys, preferred_element_type=jnp.float32
    ) * HD ** (-0.5)
    is_live = jnp.arange(CTX, dtype=jnp.int32)[None, :] < own_lengths[:, None]
    scores = jnp.where(is_live[:, None, None, :], scores, -jnp.inf)
    row_max = jnp.max(scores, axis=-1, keepdims=True)
    expsum = jnp.exp(scores - row_max)
    probs = (expsum / jnp.sum(expsum, axis=-1, keepdims=True)).astype(jnp.bfloat16)
    context = jnp.einsum(
        "tkgc,tckd->tkgd", probs, cached_values, preferred_element_type=jnp.float32
    )
    return context.astype(jnp.bfloat16).reshape(tok_dev, MODEL_WIDTH)


def solution(mesh):
    in_specs = (
        P(("segment", "adapter"), None),
        P("segment", None),
        P("segment", None, "adapter"),
        P("segment", "adapter", None, None),
        P("segment", None, None, "adapter"),
        P("segment"),
        P("segment"),
        P(("segment", "adapter"), None, None, None),
    )
    out_specs = P(("segment", "adapter"), None)
    return jax.shard_map(body, mesh=mesh, in_specs=in_specs, out_specs=out_specs, check_vma=False)
```
